32 devices in a mesh: wave: 4 (over x, core), dom: 8 (over z, y).
Axes of the slice: x: 2, y: 2, z: 4, core: 2. Of those that a mesh axis runs over, the one named last changes fastest.
Arguments:
- rhs: float32 [4, 8, 12, 32, 625], P('wave', 'dom'), may hold values from -6 to 6
- start: float32 [4, 8, 12, 32, 625], P('wave', 'dom'), may hold values from -6 to 6
- block_inv: bfloat16 [4, 8, 12, 625, 625], P('wave', 'dom'), as said below
- coup_up: bfloat16 [4, 8, 12, 3, 128, 625], P('wave', 'dom'), may hold values from -0.21875 to 0.21875
- coup_down: bfloat16 [4, 8, 12, 3, 128, 625], P('wave', 'dom'), may hold values from -0.21875 to 0.21875
- down_pick: int32 [4, 8, 8, 9], P('wave', 'dom'), may hold values from 0 to 36, as said below
- down_slot: int32 [4, 8, 36], P('wave', 'dom'), may hold values from 0 to 72, as said below
- up_pick: int32 [4, 8, 8, 9], P('wave', 'dom'), may hold values from 0 to 36, as said below
- up_slot: int32 [4, 8, 36], P('wave', 'dom'), may hold values from 0 to 72, as said below
Outputs:
- half_sweep: float32 [4, 8, 12, 32, 625], P('wave', 'dom')
- solution: float32 [4, 8, 12, 32, 625], P('wave', 'dom')
The draws below stay inside these ranges and needn't reach their ends.
Inputs may be any that keep to these rules, and one draw needn't show every extreme that they name: `block_inv`: each block is the inverse of an element's diagonal block. For l < 3, every down face of every partition s of level l appears exactly once among the used entries of down_pick[l, s]; the slots of a pair (s, d) are used from j = 0 up, and unused slots and all of level 3 hold 36. Every partition of a level below the last fills all 9 slots toward some partition. down_slot[l, d, f] = s * 9 + j names a used slot j of down_pick[l - 1, s, d]; each used slot is named by exactly one up face; level 0 holds 72. up_pick[l + 1, d, s, j] is the up face of partition d at level l + 1 joined to the down face down_pick[l, s, d, j]; unused slots and all of level 0 hold 36. up_slot[l, s, f] = d * 9 + j names a used slot j of up_pick[l + 1, d, s]; each used slot is named by exactly one down face; level 3 holds 72.
All inputs are finite; a program needn't handle non-finite values.
Results may differ from the reference program's by a relative error of at most 0.018.
Values may be sent and summed in bfloat16 or wider, within the bound.
A program may use at most 128 MiB of HBM per device.

```python
import math
import jax
import jax.numpy as jnp
from jax import lax

VARS = 5
NODES1 = 5
R = 32
E_DEV = 12
LEVELS = 4
PARTS_SIZE = 8
BLOCK = 625
FACE = 125
FTR = 128
FSLOT = 9


def connect_levels(key):
    face_count = 3 * E_DEV
    slot_count = FSLOT
    pad_slot = PARTS_SIZE * FSLOT
    down_pick = jnp.full((LEVELS, PARTS_SIZE, PARTS_SIZE, slot_count), face_count, jnp.int32)
    up_pick = jnp.full((LEVELS, PARTS_SIZE, PARTS_SIZE, slot_count), face_count, jnp.int32)
    down_slot = jnp.full((LEVELS, PARTS_SIZE, face_count), pad_slot, jnp.int32)
    up_slot = jnp.full((LEVELS, PARTS_SIZE, face_count), pad_slot, jnp.int32)
    part_ids = jnp.arange(PARTS_SIZE, dtype=jnp.int32)
    slot_ids = jnp.arange(slot_count, dtype=jnp.int32)
    face_ids = jnp.arange(face_count, dtype=jnp.int32)
    others = PARTS_SIZE - 1
    rest_total = face_count - slot_count
    for level in range(LEVELS - 1):
        keys_now = jax.random.split(jax.random.fold_in(key, level), 5)
        dest_perm = jax.random.permutation(keys_now[0], PARTS_SIZE).astype(jnp.int32)
        src_perm = jax.random.permutation(keys_now[1], PARTS_SIZE).astype(jnp.int32)
        extra_rank = jax.random.permutation(keys_now[2], others).astype(jnp.int32)
        amounts = jnp.concatenate([jnp.full((1,), slot_count, jnp.int32), rest_total // others + (extra_rank < rest_total % others).astype(jnp.int32)])
        offsets = (dest_perm[None, :] - src_perm[:, None]) % PARTS_SIZE
        counts = amounts[offsets]
        order_dest = jax.vmap(lambda one_key: jax.random.permutation(one_key, face_count))(jax.random.split(keys_now[3], PARTS_SIZE)).astype(jnp.int32)
        order_src = jax.vmap(lambda one_key: jax.random.permutation(one_key, face_count))(jax.random.split(keys_now[4], PARTS_SIZE)).astype(jnp.int32)
        start_dest = jnp.cumsum(counts, axis=0) - counts
        start_src = jnp.cumsum(counts, axis=1) - counts
        live_slot = slot_ids[None, None, :] < counts[:, :, None]
        src_pos = jnp.minimum(start_src[:, :, None] + slot_ids[None, None, :], face_count - 1)
        dest_pos = jnp.minimum(start_dest[:, :, None] + slot_ids[None, None, :], face_count - 1)
        sent_face = order_src[part_ids[:, None, None], src_pos]
        kept_face = order_dest[part_ids[None, :, None], dest_pos]
        down_pick = down_pick.at[level].set(jnp.where(live_slot, sent_face, face_count))
        up_pick = up_pick.at[level + 1].set(jnp.swapaxes(jnp.where(live_slot, kept_face, face_count), 0, 1))
        every_face = jnp.broadcast_to(face_ids[None, :], (PARTS_SIZE, face_count))
        where_dest = jnp.zeros((PARTS_SIZE, face_count), jnp.int32).at[part_ids[:, None], order_dest].set(every_face)
        end_dest = start_dest + counts
        src_of = jnp.sum((end_dest.T[:, :, None] <= where_dest[:, None, :]).astype(jnp.int32), axis=1)
        down_slot = down_slot.at[level + 1].set(src_of * slot_count + where_dest - start_dest.T[part_ids[:, None], src_of])
        where_src = jnp.zeros((PARTS_SIZE, face_count), jnp.int32).at[part_ids[:, None], order_src].set(every_face)
        end_src = start_src + counts
        dest_of = jnp.sum((end_src[:, :, None] <= where_src[:, None, :]).astype(jnp.int32), axis=1)
        up_slot = up_slot.at[level].set(dest_of * slot_count + where_src - start_src[part_ids[:, None], dest_of])
    return (down_pick, down_slot, up_pick, up_slot)


def draw_down_pick(key, part):
    return connect_levels(jax.random.fold_in(key, 11))[0]


def draw_down_slot(key, part):
    return connect_levels(jax.random.fold_in(key, 11))[1]


def draw_up_pick(key, part):
    return connect_levels(jax.random.fold_in(key, 11))[2]


def draw_up_slot(key, part):
    return connect_levels(jax.random.fold_in(key, 11))[3]


def draw_block_inv(key, part):
    shape_all = (LEVELS, PARTS_SIZE, E_DEV, BLOCK, BLOCK)
    first_key, second_key = jax.random.split(key)
    row_ids = lax.broadcasted_iota(jnp.int32, (BLOCK, BLOCK), 0)
    col_ids = lax.broadcasted_iota(jnp.int32, (BLOCK, BLOCK), 1)
    unit_matrix = jnp.where(row_ids == col_ids, 1.0, 0.0).astype(jnp.float32)
    gains = 1.0 + 0.3 * jax.random.uniform(first_key, (LEVELS, PARTS_SIZE, E_DEV, BLOCK, 1), jnp.float32, -1.0, 1.0)
    noise = jax.random.normal(second_key, shape_all, jnp.float32)
    return (unit_matrix * gains + noise * (0.6 / math.sqrt(BLOCK))).astype(jnp.bfloat16)


def level_of(key, dims, shards, smallest, largest):
    gain = 1.0
    for position, blocks in shards:
        draws = jax.random.uniform(jax.random.fold_in(jax.random.fold_in(key, 6), position), (blocks,), jnp.float32, smallest / len(shards), largest / len(shards))
        gain = gain * jnp.repeat(jnp.exp(draws), dims[position] // blocks).reshape((-1,) + (1,) * (len(dims) - 1 - position))
    return gain


def scatter_about(stream_key, extent, scale, reach, cuts=(), held_as=jnp.bfloat16):
    values = jax.random.normal(stream_key, extent, jnp.float32) * scale
    if len(cuts) > 0:
        values = level_of(stream_key, extent, cuts, -0.22, 0.18) * values
    return jnp.clip(values, min=-reach, max=reach).astype(held_as)


def setup_inputs(seed: int = 0) -> dict:
    key_of = jax.random.split(jax.random.key(seed), 10)
    rhs = scatter_about(key_of[0], (LEVELS, PARTS_SIZE, E_DEV, R, BLOCK), 1.0, 6.0, ((0, 4), (1, 8)), jnp.float32)
    start = scatter_about(key_of[1], (LEVELS, PARTS_SIZE, E_DEV, R, BLOCK), 1.0, 6.0, ((0, 4), (1, 8)), jnp.float32)
    block_inv = draw_block_inv(jax.random.fold_in(key_of[9], 71), 0)
    coup_up = scatter_about(key_of[3], (LEVELS, PARTS_SIZE, E_DEV, 3, FTR, BLOCK), (6 * FTR) ** -0.5, 0.21875, ((0, 4), (1, 8)))
    coup_down = scatter_about(key_of[4], (LEVELS, PARTS_SIZE, E_DEV, 3, FTR, BLOCK), (6 * FTR) ** -0.5, 0.21875, ((0, 4), (1, 8)))
    down_pick = draw_down_pick(jax.random.fold_in(key_of[9], 71), 0)
    down_slot = draw_down_slot(jax.random.fold_in(key_of[9], 71), 0)
    up_pick = draw_up_pick(jax.random.fold_in(key_of[9], 71), 0)
    up_slot = draw_up_slot(jax.random.fold_in(key_of[9], 71), 0)
    return {"rhs": rhs, "start": start, "block_inv": block_inv, "coup_up": coup_up, "coup_down": coup_down, "down_pick": down_pick, "down_slot": down_slot, "up_pick": up_pick, "up_slot": up_slot}


def face_traces(field, face_side):
    lead_dims = field.shape[:-1]
    cube = field.reshape(lead_dims + (VARS, NODES1, NODES1, NODES1))
    edge_at = 0 if face_side == 0 else NODES1 - 1
    three_faces = [cube[..., edge_at, :, :], cube[..., :, edge_at, :], cube[..., :, :, edge_at]]
    flat_faces = [one_face.reshape(lead_dims + (FACE,)) for one_face in three_faces]
    stacked = jnp.stack(flat_faces, axis=-3)
    padding = [(0, 0)] * (stacked.ndim - 1) + [(0, FTR - FACE)]
    padded = jnp.pad(stacked, padding).astype(jnp.bfloat16)
    shape_now = padded.shape
    return padded.reshape(shape_now[:-4] + (shape_now[-4] * 3,) + shape_now[-2:])


def route_faces(sender_traces, pick_list, slot_list):
    parts_all = sender_traces.shape[0]
    blank = jnp.zeros((parts_all, 1) + sender_traces.shape[2:], jnp.bfloat16)
    extended = jnp.concatenate([sender_traces, blank], axis=1)
    sources = jnp.arange(parts_all, dtype=jnp.int32)[:, None, None]
    outgoing = extended[sources, pick_list]
    incoming = jnp.swapaxes(outgoing, 0, 1).reshape((parts_all, -1) + sender_traces.shape[2:])
    incoming = jnp.concatenate([incoming, blank], axis=1)
    receivers = jnp.arange(parts_all, dtype=jnp.int32)[:, None]
    return incoming[receivers, slot_list]


def couple_faces(neighbours, coupling):
    def one_part(pair_now):
        near_faces, weights = pair_now
        near_faces = near_faces.reshape(weights.shape[0], 3, near_faces.shape[1], near_faces.shape[2]).astype(jnp.float32)
        return jnp.einsum("ekrt,ektb->erb", near_faces, weights.astype(jnp.float32))
    return lax.map(one_part, (neighbours, coupling))


def relax_level(rhs_level, first_near, first_coup, second_near, second_coup, inverse):
    partial_sum = rhs_level - couple_faces(first_near, first_coup)
    residual = (partial_sum - couple_faces(second_near, second_coup)).astype(jnp.bfloat16)

    def apply_inverse(pair_now):
        rows_now, inverse_now = pair_now
        return jnp.einsum("eri,eij->erj", rows_now.astype(jnp.float32), inverse_now.astype(jnp.float32))
    return lax.map(apply_inverse, (residual, inverse))


def reference(rhs, start, block_inv, coup_up, coup_down, down_pick, down_slot, up_pick, up_slot):
    blank_near = jnp.zeros((PARTS_SIZE, 3 * E_DEV, R, FTR), jnp.bfloat16)
    lower_old = []
    for level in range(LEVELS):
        if level < LEVELS - 1:
            lower_old.append(route_faces(face_traces(start[level + 1], 0), up_pick[level + 1], up_slot[level]))
        else:
            lower_old.append(blank_near)
    upper_new = [blank_near]
    half_sweep = []
    for level in range(LEVELS):
        field_now = relax_level(rhs[level], lower_old[level], coup_down[level], upper_new[level], coup_up[level], block_inv[level])
        half_sweep.append(field_now)
        if level < LEVELS - 1:
            upper_new.append(route_faces(face_traces(field_now, 1), down_pick[level], down_slot[level + 1]))
    solution = [None] * LEVELS
    solution[LEVELS - 1] = half_sweep[LEVELS - 1]
    for level in range(LEVELS - 2, -1, -1):
        lower_new = route_faces(face_traces(solution[level + 1], 0), up_pick[level + 1], up_slot[level])
        solution[level] = relax_level(rhs[level], upper_new[level], coup_up[level], lower_new, coup_down[level], block_inv[level])
    return jnp.stack(half_sweep), jnp.stack(solution)
```

```python
import functools

import jax
import jax.numpy as jnp
import numpy as np
from jax import lax
from jax.experimental import pallas as pl
from jax.experimental.pallas import tpu as pltpu
from jax.sharding import PartitionSpec as P

VARS = 5
NODES1 = 5
FACE = 125
FTR = 128
MESH = pl.DeviceIdType.MESH
F32 = jnp.float32
BF16 = jnp.bfloat16


def face_columns():
    columns = np.full((8, FTR), -1, np.int32)
    t = np.arange(FACE)
    var, i, j = t // 25, (t // 5) % 5, t % 5
    for side in range(2):
        edge = 0 if side == 0 else NODES1 - 1
        columns[3 * side + 0, :FACE] = var * 125 + edge * 25 + i * 5 + j
        columns[3 * side + 1, :FACE] = var * 125 + i * 25 + edge * 5 + j
        columns[3 * side + 2, :FACE] = var * 125 + i * 25 + j * 5 + edge
    return columns


def kernel(
    levels, parts,
    rhs_h, start_h, inv_h, cup_h, cdn_h, dpick, dslot, upick, uslot, cols,
    half_h, sol_h,
    rhs_v, work_v, half_v, inv_v, cup_v, cdn_v, mup_v, mdn_v, rb_v, sel_v, faces_v,
    send_old, send_up, send_low, recv_old, recv_up, recv_low,
    load_sem, inv_sem, cup_sem, cdn_sem, out_sem, ssem, rsem,
):
    wave = lax.axis_index("wave")
    dom = lax.axis_index("dom")
    elems, rows, block = rhs_v.shape
    slots = dpick.shape[1]
    nslot = parts * slots
    nface = 3 * elems
    first = wave == 0
    last = wave == levels - 1

    start_copy = pltpu.make_async_copy(start_h, work_v, load_sem.at[0])
    start_copy.start()
    rhs_copy = pltpu.make_async_copy(rhs_h, rhs_v, load_sem.at[1])
    rhs_copy.start()
    inv_copy = lambda e: pltpu.make_async_copy(inv_h.at[e], inv_v.at[e], inv_sem.at[e])
    cdn_copy = lambda e: pltpu.make_async_copy(cdn_h.at[e], cdn_v.at[e], cdn_sem.at[e])
    cup_copy = lambda e: pltpu.make_async_copy(cup_h.at[e], cup_v.at[e], cup_sem.at[e])
    for e in range(elems):
        inv_copy(e).start()
        cdn_copy(e).start()
    for e in range(elems):
        cup_copy(e).start()

    barrier = pltpu.get_barrier_semaphore()

    def greet(to):
        @pl.loop(0, parts)
        def _(d):
            pl.semaphore_signal(barrier, inc=1, device_id=(to, d), device_id_type=MESH)

    pl.when(wave > 0)(lambda: greet(wave - 1))
    pl.when(wave < levels - 1)(lambda: greet(wave + 1))

    zero = jnp.zeros((rows, FTR), BF16)
    faces_v[nface] = zero
    recv_old[nslot] = zero
    recv_up[nslot] = zero
    recv_low[nslot] = zero
    row_ids = lax.broadcasted_iota(jnp.int32, (block, FTR), 0)
    for q in range(6):
        hit = row_ids == jnp.broadcast_to(cols[q : q + 1, :], (block, FTR))
        sel_v[q // 3, :, (q % 3) * FTR : (q % 3 + 1) * FTR] = jnp.where(hit, 1.0, 0.0).astype(BF16)

    def traces(field, side):
        flat = field[...].reshape(elems * rows, block).astype(BF16)
        got = jnp.dot(flat, sel_v[side], preferred_element_type=F32).astype(BF16)
        for e in range(elems):
            for k in range(3):
                faces_v[3 * e + k] = got[e * rows : (e + 1) * rows, k * FTR : (k + 1) * FTR]

    def copy_to(phase, send, recv, to, d):
        return pltpu.make_async_remote_copy(
            src_ref=send.at[pl.ds(d * slots, slots)],
            dst_ref=recv.at[pl.ds(dom * slots, slots)],
            send_sem=ssem.at[phase, d],
            recv_sem=rsem.at[phase, dom],
            device_id=(to, d),
            device_id_type=MESH,
        )

    def send_all(phase, pick, send, recv, to):
        @pl.loop(0, parts)
        def _(i):
            d = lax.rem(dom + parts // 2 + i, parts)
            for j in range(slots):
                send[d * slots + j] = faces_v[pick[d, j]]
            copy_to(phase, send, recv, to, d).start()

    def finish_send(phase, send, recv, to):
        @pl.loop(0, parts)
        def _(d):
            copy_to(phase, send, recv, to, d).wait_send()

    def finish_recv(phase, send, recv, source):
        @pl.loop(0, parts)
        def _(s):
            pltpu.make_async_remote_copy(
                src_ref=send.at[pl.ds(s * slots, slots)],
                dst_ref=recv.at[pl.ds(s * slots, slots)],
                send_sem=ssem.at[phase, s],
                recv_sem=rsem.at[phase, s],
                device_id=(source, s),
                device_id_type=MESH,
            ).wait_recv()

    def near(recv, slot, e):
        return jnp.concatenate([recv[slot[3 * e + k]] for k in range(3)], axis=1)

    def fold(c_v, m_v, e):
        three = jnp.concatenate([c_v[e, k] for k in range(3)], axis=1)
        m_v[e] = lax.dot_general(
            three, inv_v[e], (((0,), (0,)), ((), ())), preferred_element_type=F32
        ).astype(BF16)

    start_copy.wait()
    traces(work_v, 0)

    sides = jnp.where(first, 0, 1) + jnp.where(last, 0, 1)
    pl.semaphore_wait(barrier, parts * sides)
    pl.when(wave > 0)(lambda: send_all(0, upick, send_old, recv_old, wave - 1))

    rhs_copy.wait()

    @pl.loop(0, elems)
    def _(e):
        inv_copy(e).wait()
        cdn_copy(e).wait()
        rb_v[e] = jnp.dot(rhs_v[e].astype(BF16), inv_v[e], preferred_element_type=F32)
        half_v[e] = rb_v[e]

        @pl.when(wave < levels - 1)
        def _():
            fold(cdn_v, mdn_v, e)

    @pl.when(wave < levels - 1)
    def _():
        finish_recv(0, send_old, recv_old, wave + 1)

        @pl.loop(0, elems)
        def _(e):
            half_v[e] = rb_v[e] - jnp.dot(near(recv_old, uslot, e), mdn_v[e], preferred_element_type=F32)

    @pl.loop(0, elems)
    def _(e):
        cup_copy(e).wait()

    @pl.when(wave > 0)
    def _():
        @pl.loop(0, elems)
        def _(e):
            fold(cup_v, mup_v, e)

        finish_recv(1, send_up, recv_up, wave - 1)

        @pl.loop(0, elems)
        def _(e):
            term = jnp.dot(near(recv_up, dslot, e), mup_v[e], preferred_element_type=F32)
            half_v[e] = half_v[e] - term
            rb_v[e] = rb_v[e] - term

    @pl.when(wave < levels - 1)
    def _():
        traces(half_v, 1)
        send_all(1, dpick, send_up, recv_up, wave + 1)

    half_copy = pltpu.make_async_copy(half_v, half_h, out_sem.at[0])
    half_copy.start()

    @pl.when(last)
    def _():
        work_v[...] = half_v[...]

    @pl.when(wave < levels - 1)
    def _():
        finish_recv(2, send_low, recv_low, wave + 1)

        @pl.loop(0, elems)
        def _(e):
            work_v[e] = rb_v[e] - jnp.dot(near(recv_low, uslot, e), mdn_v[e], preferred_element_type=F32)

    @pl.when(wave > 0)
    def _():
        traces(work_v, 0)
        send_all(2, upick, send_low, recv_low, wave - 1)

    sol_copy = pltpu.make_async_copy(work_v, sol_h, out_sem.at[1])
    sol_copy.start()

    @pl.when(wave > 0)
    def _():
        finish_send(0, send_old, recv_old, wave - 1)
        finish_send(2, send_low, recv_low, wave - 1)

    @pl.when(wave < levels - 1)
    def _():
        finish_send(1, send_up, recv_up, wave + 1)

    half_copy.wait()
    sol_copy.wait()


def local(rhs, start, block_inv, coup_up, coup_down, down_pick, down_slot, up_pick, up_slot):
    levels, parts = lax.axis_size("wave"), lax.axis_size("dom")
    elems, rows, block = rhs.shape[2:]
    slots = down_pick.shape[-1]
    nslot = parts * slots
    field = jax.ShapeDtypeStruct((elems, rows, block), F32)
    anywhere = pl.BlockSpec(memory_space=pl.ANY)
    scalar = pl.BlockSpec(memory_space=pltpu.SMEM)
    fold_shape = (elems, 3 * FTR, block)
    coup_shape = (elems, 3, block, FTR)
    half, final = pl.pallas_call(
        functools.partial(kernel, levels, parts),
        out_shape=(field, field),
        in_specs=[anywhere] * 5 + [scalar] * 4 + [pl.BlockSpec(memory_space=pltpu.VMEM)],
        out_specs=(anywhere, anywhere),
        scratch_shapes=[
            pltpu.VMEM((elems, rows, block), F32),
            pltpu.VMEM((elems, rows, block), F32),
            pltpu.VMEM((elems, rows, block), F32),
            pltpu.VMEM((elems, block, block), BF16),
            pltpu.VMEM(coup_shape, BF16),
            pltpu.VMEM(coup_shape, BF16),
            pltpu.VMEM(fold_shape, BF16),
            pltpu.VMEM(fold_shape, BF16),
            pltpu.VMEM((elems, rows, block), F32),
            pltpu.VMEM((2, block, 3 * FTR), BF16),
            pltpu.VMEM((3 * elems + 1, rows, FTR), BF16),
        ]
        + [pltpu.VMEM((nslot, rows, FTR), BF16)] * 3
        + [pltpu.VMEM((nslot + 1, rows, FTR), BF16)] * 3
        + [
            pltpu.SemaphoreType.DMA((2,)),
            pltpu.SemaphoreType.DMA((elems,)),
            pltpu.SemaphoreType.DMA((elems,)),
            pltpu.SemaphoreType.DMA((elems,)),
            pltpu.SemaphoreType.DMA((2,)),
            pltpu.SemaphoreType.DMA((3, parts)),
            pltpu.SemaphoreType.DMA((3, parts)),
        ],
        compiler_params=pltpu.CompilerParams(
            collective_id=0, has_side_effects=True, vmem_limit_bytes=62 * 1024 * 1024
        ),
    )(
        rhs[0, 0],
        start[0, 0],
        block_inv[0, 0],
        jnp.swapaxes(coup_up[0, 0], -1, -2),
        jnp.swapaxes(coup_down[0, 0], -1, -2),
        down_pick[0, 0],
        down_slot[0, 0],
        up_pick[0, 0],
        up_slot[0, 0],
        jnp.asarray(face_columns()),
    )
    return (half[None, None], final[None, None])


def solution(mesh):
    placed = (
        P("wave", "dom", None, None, None),
        P("wave", "dom", None, None, None),
        P("wave", "dom", None, None, None),
        P("wave", "dom", None, None, None, None),
        P("wave", "dom", None, None, None, None),
        P("wave", "dom", None, None),
        P("wave", "dom", None),
        P("wave", "dom", None, None),
        P("wave", "dom", None),
    )
    return jax.shard_map(
        local,
        mesh=mesh,
        in_specs=placed,
        out_specs=(P("wave", "dom", None, None, None), P("wave", "dom", None, None, None)),
        check_vma=False,
    )
```
